32 devices in a mesh: gx: 4 (over x, core), gy: 8 (over z, y).
Axes of the slice: x: 2, y: 2, z: 4, core: 2. Of those that a mesh axis runs over, the one named last changes fastest.
Arguments:
- snapshots: bfloat16 [2, 8192, 8192], P(None, 'gx', 'gy'), may hold values from -200 to 200
- mode_one_test: bfloat16 [2, 8192, 128], P(None, 'gy'), may hold values from -0.148231765 to 0.148231765
- mode_two_test: bfloat16 [2, 8192, 128], P(None, 'gx'), may hold values from -0.046875 to 0.046875
- row_sketch: bfloat16 [256, 8192], P(None, 'gx'), may hold values from -0.0625 to 0.0625
- column_sketch: bfloat16 [256, 8192], P(None, 'gy'), may hold values from -0.0625 to 0.0625
- old_mode_one: float32 [8192, 128], P('gx'), may hold values from -3 to 3
- old_mode_two: float32 [8192, 128], P('gy'), may hold values from -3 to 3
- old_core: float32 [9, 256, 256], replicated, may hold values from -3 to 3
- time_mix: float32 [9, 2], replicated, may hold values from -2.5 to 2.5
Outputs:
- basis: float32 [8192, 128], P(('gx', 'gy'))
- mode_two: float32 [8192, 128], P('gy')
- projected: float32 [128, 2, 8192], P('gx', None, 'gy')
- core: float32 [9, 256, 256], replicated
The draws below stay inside these ranges and needn't reach their ends.
All inputs are finite; a program needn't handle non-finite values.
Results may differ from the reference program's by a relative error of at most 0.0024.
Values may be sent and summed in bfloat16 or wider, within the bound.
No kernel may reach another device: no remote copies, remote signals or barrier semaphores. Data moves between devices by JAX's collectives and lax.ppermute only.
A program may use at most 128 MiB of HBM per device.

```python
import math
import jax
import jax.numpy as jnp
from jax import lax

K = 128
S = 256
TS = 9
N1 = 8192
N2 = 8192


def draw_snapshots(key, part):
    keys = jax.random.split(jax.random.fold_in(key, 11), 3)
    row_pos = jnp.arange(N1, dtype=jnp.float32) / N1
    col_pos = jnp.arange(N2, dtype=jnp.float32) / N2
    row_scale = jnp.exp(math.log(3.0) * row_pos + jax.random.uniform(keys[0], (N1,), jnp.float32, 0.0, math.log(10.0 / 3.0)))
    col_scale = jnp.exp(math.log(3.0) * col_pos + jax.random.uniform(keys[1], (N2,), jnp.float32, 0.0, math.log(10.0 / 3.0)))
    noise = jnp.clip(jax.random.normal(keys[2], (2, N1, N2), jnp.float32), -6.0, 6.0)
    values = noise * row_scale[None, :, None] * col_scale[None, None, :] / 3.0
    return values.astype(jnp.bfloat16)


def draw_mode_one_test(key, part):
    keys = jax.random.split(jax.random.fold_in(key, 23), 2)
    col_scale = jnp.exp(jax.random.uniform(keys[0], (K,), jnp.float32, 0.0, math.log(10.0)))
    noise = jnp.clip(jax.random.normal(keys[1], (2, N2, K), jnp.float32), -6.0, 6.0)
    values = noise * col_scale[None, None, :] / math.sqrt(20.0 * N2)
    return values.astype(jnp.bfloat16)


def shard_levels(stream_key, shape, cuts, least, largest):
    def one(position, blocks):
        draws = jax.random.uniform(jax.random.fold_in(jax.random.fold_in(stream_key, 6), position), (blocks,), jnp.float32, least / len(cuts), largest / len(cuts))
        return jnp.repeat(jnp.exp(draws), shape[position] // blocks).reshape((-1,) + (1,) * (len(shape) - position - 1))

    loudness = one(*cuts[0])
    for cut in cuts[1:]:
        loudness = loudness * one(*cut)
    return loudness


def bell_draw(rng, shape, width, limit, cuts=(), kind=jnp.bfloat16):
    loudness = shard_levels(rng, shape, cuts, -0.22, 0.18) if cuts else 1.0
    result = jax.random.normal(rng, shape, jnp.float32) * width * loudness
    return jnp.minimum(jnp.maximum(result, -limit), limit).astype(kind)


def setup_inputs(seed: int = 0) -> dict:
    streams_of = jax.random.split(jax.random.key(seed), 10)
    snapshots = draw_snapshots(jax.random.fold_in(streams_of[9], 71), 0)
    mode_one_test = draw_mode_one_test(jax.random.fold_in(streams_of[9], 71), 0)
    mode_two_test = bell_draw(streams_of[2], (2, N1, K), (2 * N1) ** -0.5, 0.046875, ((1, 4),))
    row_sketch = bell_draw(streams_of[3], (S, N1), N1 ** -0.5, 0.0625, ((1, 4),))
    column_sketch = bell_draw(streams_of[4], (S, N2), N2 ** -0.5, 0.0625, ((1, 8),))
    old_mode_one = bell_draw(streams_of[5], (N1, K), 0.5, 3.0, ((0, 4),), jnp.float32)
    old_mode_two = bell_draw(streams_of[6], (N2, K), 0.5, 3.0, ((0, 8),), jnp.float32)
    old_core = bell_draw(streams_of[7], (TS, S, S), 0.5, 3.0, (), jnp.float32)
    time_mix = bell_draw(streams_of[8], (TS, 2), 0.7, 2.5, (), jnp.float32)
    return dict(snapshots=snapshots, mode_one_test=mode_one_test, mode_two_test=mode_two_test, row_sketch=row_sketch, column_sketch=column_sketch, old_mode_one=old_mode_one, old_mode_two=old_mode_two, old_core=old_core, time_mix=time_mix)


def reference(snapshots, mode_one_test, mode_two_test, row_sketch, column_sketch, old_mode_one, old_mode_two, old_core, time_mix):
    root_rows = math.sqrt(N1)
    mode_one = old_mode_one
    mode_two = old_mode_two
    slices = []
    column_wide = column_sketch.astype(jnp.float32)
    for moment in range(2):
        layer = snapshots[moment]
        mode_one = mode_one + jnp.dot(layer.astype(jnp.float32), mode_one_test[moment].astype(jnp.float32), preferred_element_type=jnp.float32)
        mode_two = mode_two + jnp.dot(layer.T.astype(jnp.float32), mode_two_test[moment].astype(jnp.float32), preferred_element_type=jnp.float32)
        folded = jnp.dot(row_sketch.astype(jnp.float32), layer.astype(jnp.float32), preferred_element_type=jnp.float32)
        slices.append(jnp.dot(folded, column_wide.T, precision=lax.Precision.HIGHEST))
    stacked = jnp.stack(slices)
    core = old_core + jnp.einsum('jt,tsu->jsu', time_mix, stacked, precision=lax.Precision.HIGHEST)
    gram_matrix = jnp.dot(mode_one.T, mode_one, precision=lax.Precision.HIGHEST)
    factor = jnp.linalg.cholesky(gram_matrix)
    basis = root_rows * jax.scipy.linalg.solve_triangular(factor, mode_one.T, lower=True).T
    basis_low = basis.astype(jnp.bfloat16)
    pieces = [jnp.dot(basis_low.T.astype(jnp.float32), snapshots[moment].astype(jnp.float32), preferred_element_type=jnp.float32) for moment in range(2)]
    projected = jnp.stack(pieces, axis=1) / root_rows
    return (basis, mode_two, projected, core)
```

```python
import functools
import math

import jax
import jax.numpy as jnp
from jax import lax
from jax.experimental import pallas as pl
from jax.experimental.pallas import tpu as pltpu
from jax.sharding import PartitionSpec as P

HIGHEST = lax.Precision.HIGHEST
F32 = jnp.float32
BF16 = jnp.bfloat16


def exchange(value, axis, bit):
    size = lax.axis_size(axis)
    return lax.ppermute(value, axis, [(i, i ^ bit) for i in range(size)])


def bits_of(size):
    return [1 << i for i in range(size.bit_length() - 1)]


def mode_one_kernel(order_ref, snap_ref, test_ref, out_ref):
    moments = snap_ref.shape[0]
    total = jnp.dot(snap_ref[0], test_ref[0], preferred_element_type=F32)
    for t in range(1, moments):
        total += jnp.dot(snap_ref[t], test_ref[t], preferred_element_type=F32)
    out_ref[0] = total


def mode_one_blocks(order, count, snapshots, test, block):
    moments, rows, cols = snapshots.shape
    rank = test.shape[2]
    return pl.pallas_call(
        mode_one_kernel,
        grid_spec=pltpu.PrefetchScalarGridSpec(
            num_scalar_prefetch=1,
            grid=(count,),
            in_specs=[
                pl.BlockSpec((moments, block, cols), lambda i, o: (0, o[i], 0)),
                pl.BlockSpec((moments, cols, rank), lambda i, o: (0, 0, 0)),
            ],
            out_specs=pl.BlockSpec((1, block, rank), lambda i, o: (i, 0, 0)),
        ),
        out_shape=jax.ShapeDtypeStruct((count, block, rank), F32),
        cost_estimate=pl.CostEstimate(
            flops=2 * moments * count * block * cols * rank,
            bytes_accessed=2 * moments * count * block * cols,
            transcendentals=0,
        ),
        name="mode_one",
    )(order, snapshots, test)


def gram_kernel(order_ref, mine_ref, other_ref, old_ref, rows_ref, gram_ref):
    value = mine_ref[0] + other_ref[0] + old_ref[...]
    rows_ref[0] = value
    term = lax.dot_general(
        value, value, (((0,), (0,)), ((), ())), precision=HIGHEST, preferred_element_type=F32
    )

    @pl.when(pl.program_id(0) == 0)
    def _():
        gram_ref[...] = term

    @pl.when(pl.program_id(0) > 0)
    def _():
        gram_ref[...] += term


def finish_rows(order, mine, other, old):
    count, block, rank = mine.shape
    return pl.pallas_call(
        gram_kernel,
        grid_spec=pltpu.PrefetchScalarGridSpec(
            num_scalar_prefetch=1,
            grid=(count,),
            in_specs=[
                pl.BlockSpec((1, block, rank), lambda i, o: (i, 0, 0)),
                pl.BlockSpec((1, block, rank), lambda i, o: (count - 1 - i, 0, 0)),
                pl.BlockSpec((block, rank), lambda i, o: (o[i], 0)),
            ],
            out_specs=[
                pl.BlockSpec((1, block, rank), lambda i, o: (i, 0, 0)),
                pl.BlockSpec((rank, rank), lambda i, o: (0, 0)),
            ],
        ),
        out_shape=[
            jax.ShapeDtypeStruct((count, block, rank), F32),
            jax.ShapeDtypeStruct((rank, rank), F32),
        ],
        name="gram",
    )(order, mine, other, old)


def inverse_factor_kernel(gram_ref, inverse_ref):
    size = gram_ref.shape[0]
    groups = size // 8
    left = [gram_ref[8 * q : 8 * q + 8, :] for q in range(groups)]
    row = lax.broadcasted_iota(jnp.int32, (8, size), 0)
    column = lax.broadcasted_iota(jnp.int32, (8, size), 1)
    right = [jnp.where(column == row + 8 * q, 1.0, 0.0).astype(F32) for q in range(groups)]
    for p in range(groups):
        pivots = jnp.zeros((8, size), F32)
        for i in range(8):
            c = 8 * p + i
            left_row = jnp.broadcast_to(left[p][i : i + 1, :], (8, size))
            right_row = jnp.broadcast_to(right[p][i : i + 1, :], (8, size))
            pivot = jnp.broadcast_to(left_row[:, c : c + 1], (8, size))
            inverse = 1.0 / pivot
            left_row = left_row * inverse
            right_row = right_row * inverse
            pivots = jnp.where(row == i, pivot, pivots)
            for q in range(p, groups):
                factor = jnp.broadcast_to(left[q][:, c : c + 1], (8, size))
                if q == p:
                    factor = jnp.where(row > i, factor, 0.0)
                left[q] = left[q] - factor * left_row
                right[q] = right[q] - factor * right_row
        inverse_ref[8 * p : 8 * p + 8, :] = right[p] * lax.rsqrt(pivots)


def inverse_factor(gram):
    return pl.pallas_call(
        inverse_factor_kernel,
        out_shape=jax.ShapeDtypeStruct(gram.shape, F32),
        cost_estimate=pl.CostEstimate(flops=10_000_000, bytes_accessed=131072, transcendentals=0),
        name="inverse_factor",
    )(gram)


def basis_kernel(root_rows, parts, place_ref, inverse_ref, *refs):
    pieces = refs[:parts]
    low_ref, own_ref, turned = refs[parts:]
    own_ref[...] = root_rows * lax.dot_general(
        pieces[0][0], inverse_ref[...], (((1,), (1,)), ((), ())), precision=HIGHEST,
        preferred_element_type=F32,
    )
    shares = place_ref.shape[0]
    share = inverse_ref.shape[0] // shares
    for k in range(shares):
        start = pl.multiple_of(place_ref[k] * share, share)
        turned[k * share : (k + 1) * share, :] = inverse_ref[pl.ds(start, share), :]
    at = 0
    for piece in pieces:
        count, block, rank = piece.shape
        value = root_rows * lax.dot_general(
            piece[...].reshape(count * block, rank), turned[...], (((1,), (1,)), ((), ())),
            precision=HIGHEST, preferred_element_type=F32,
        )
        low_ref[at : at + count] = value.astype(BF16).reshape(count, block, rank)
        at += count


def basis_rows(place, inverse, pieces, root_rows):
    count = sum(p.shape[0] for p in pieces)
    _, block, rank = pieces[0].shape
    vmem = pl.BlockSpec(memory_space=pltpu.VMEM)
    return pl.pallas_call(
        functools.partial(basis_kernel, root_rows, len(pieces)),
        in_specs=[pl.BlockSpec(memory_space=pltpu.SMEM), vmem] + [vmem] * len(pieces),
        out_specs=[vmem, vmem],
        out_shape=[
            jax.ShapeDtypeStruct((count, block, rank), BF16),
            jax.ShapeDtypeStruct((block, rank), F32),
        ],
        scratch_shapes=[pltpu.VMEM((rank, rank), F32)],
        name="basis",
    )(place, inverse, *pieces)


def project_kernel(order_ref, basis_ref, snap_ref, out_ref):
    term = lax.dot_general(
        basis_ref[0], snap_ref[0], (((0,), (0,)), ((), ())), preferred_element_type=F32
    )

    @pl.when(pl.program_id(0) == 0)
    def _():
        out_ref[...] = term

    @pl.when(pl.program_id(0) > 0)
    def _():
        out_ref[...] += term


def project(order, basis_low, snapshots, moment):
    count, block, rank = basis_low.shape
    cols = snapshots.shape[2]
    return pl.pallas_call(
        project_kernel,
        grid_spec=pltpu.PrefetchScalarGridSpec(
            num_scalar_prefetch=1,
            grid=(count,),
            in_specs=[
                pl.BlockSpec((1, block, rank), lambda i, o: (i, 0, 0)),
                pl.BlockSpec((1, block, cols), lambda i, o: (moment, o[i], 0)),
            ],
            out_specs=pl.BlockSpec((rank, cols), lambda i, o: (0, 0)),
        ),
        out_shape=jax.ShapeDtypeStruct((rank, cols), F32),
        cost_estimate=pl.CostEstimate(
            flops=2 * count * block * cols * rank,
            bytes_accessed=2 * count * block * cols,
            transcendentals=0,
        ),
        name="project",
    )(order, basis_low, snapshots)


def scatter_sum(parts, axis, bits):
    parts = dict(parts)
    for bit in bits:
        sent = [j for j in sorted(parts) if j & bit]
        moved = exchange(jnp.stack([parts[j] for j in sent]), axis, bit)
        for n, j in enumerate(sent):
            parts[j ^ bit] = parts[j ^ bit] + moved[n]
            del parts[j]
    return parts[0]


def gather_all(value, axis, bits):
    parts = {0: value}
    for bit in bits:
        have = sorted(parts)
        moved = exchange(jnp.stack([parts[j] for j in have]), axis, bit)
        for n, j in enumerate(have):
            parts[j ^ bit] = moved[n]
    return parts


def body(
    snapshots,
    mode_one_test,
    mode_two_test,
    row_sketch,
    column_sketch,
    old_mode_one,
    old_mode_two,
    old_core,
    time_mix,
):
    moments, tile_rows, tile_cols = snapshots.shape
    rank = mode_one_test.shape[2]
    wide, deep = lax.axis_size("gx"), lax.axis_size("gy")
    across, along = lax.axis_index("gx"), lax.axis_index("gy")
    bits_x, bits_y = bits_of(wide), bits_of(deep)
    root_rows = math.sqrt(tile_rows * wide)
    block = tile_rows // deep

    scatter_bits, last = bits_y[:-1], bits_y[-1]
    first, rest = scatter_bits[0], scatter_bits[1:]

    def blocks(names):
        order = jnp.array(names, jnp.int32) ^ along
        return mode_one_blocks(order, len(names), snapshots, mode_one_test, block)

    names = range(deep)
    early = [j for j in names if j & first and j & rest[0]]
    late = [j for j in names if j & first and not j & rest[0]]
    kept = [j ^ first for j in early] + [j ^ first for j in late]
    early_sent = exchange(blocks(early), "gy", first)
    late_sent = exchange(blocks(late), "gy", first)
    held = blocks(kept)
    half = len(early)
    high = held[:half] + early_sent
    low = held[half:] + late_sent
    high_names, low_names = kept[:half], kept[half:]
    low = low + exchange(high, "gy", rest[0])
    for bit in rest[1:]:
        keep = [n for n, j in enumerate(low_names) if not j & bit]
        send = [low_names.index(low_names[n] ^ bit) for n in keep]
        moved = exchange(jnp.stack([low[n] for n in send]), "gy", bit)
        low = jnp.stack([low[n] for n in keep]) + moved
        low_names = [low_names[n] for n in keep]
    other = exchange(low, "gy", last)
    own_order = jnp.array(low_names, jnp.int32) ^ along
    own_rows, gram = finish_rows(own_order, low, other, old_mode_one)

    for bit in bits_x:
        gram = gram + exchange(gram, "gx", bit)
    for bit in reversed(scatter_bits):
        gram = gram + exchange(gram, "gy", bit)
    pieces = [own_rows]
    piece_names = list(low_names)
    for bit in reversed(scatter_bits):
        pieces = pieces + [exchange(p, "gy", bit) for p in pieces]
        piece_names = piece_names + [j ^ bit for j in piece_names]
    inverse = inverse_factor(gram)
    place = jnp.arange(wide, dtype=jnp.int32) ^ across
    basis_low, basis_out = basis_rows(place, inverse, pieces, root_rows)
    order = jnp.array(piece_names, jnp.int32) ^ along
    share = rank // wide
    projected = []
    for t in range(moments):
        part = project(order, basis_low, snapshots, t)
        part = {j: part[j * share : (j + 1) * share] for j in range(wide)}
        projected.append(scatter_sum(part, "gx", bits_x))
    projected = jnp.stack(projected, axis=1) / root_rows

    part_two = jnp.einsum(
        "trc,trk->ck", snapshots, mode_two_test, preferred_element_type=F32
    )
    folded = jnp.einsum("sr,trc->tsc", row_sketch, snapshots, preferred_element_type=F32)
    core_part = jnp.einsum(
        "tsc,uc->tsu", folded, column_sketch.astype(F32), precision=HIGHEST
    )
    core_shape = core_part.shape
    two = part_two.reshape(wide, -1, rank)
    flat = core_part.reshape(wide, -1, rank)
    both = jnp.concatenate([two, flat], axis=1)
    cut = two.shape[1]
    terms = {j: lax.dynamic_index_in_dim(both, across ^ j, 0, False) for j in range(wide)}
    summed = scatter_sum(terms, "gx", bits_x)
    core_rows = summed[cut:]
    size = core_rows.shape[0] // 2
    low_half = along & 1
    keep = lax.dynamic_slice_in_dim(core_rows, low_half * size, size, 0)
    send = lax.dynamic_slice_in_dim(core_rows, (1 - low_half) * size, size, 0)
    keep = keep + exchange(send, "gy", bits_y[0])
    for bit in bits_y[1:]:
        keep = keep + exchange(keep, "gy", bit)
    away = exchange(keep, "gy", bits_y[0])
    core_rows = jnp.where(
        low_half == 0, jnp.concatenate([keep, away]), jnp.concatenate([away, keep])
    )
    full = gather_all(jnp.concatenate([summed[:cut], core_rows]), "gx", list(reversed(bits_x)))
    full = jnp.stack([full[j] for j in range(wide)])
    full = jnp.stack([lax.dynamic_index_in_dim(full, across ^ j, 0, False) for j in range(wide)])
    mode_two = old_mode_two + full[:, :cut].reshape(old_mode_two.shape)
    stacked = full[:, cut:].reshape(core_shape)
    core = old_core + jnp.einsum("jt,tsu->jsu", time_mix, stacked, precision=HIGHEST)
    return (basis_out, mode_two, projected, core)


def solution(mesh):
    placed = (
        P(None, "gx", "gy"),
        P(None, "gy", None),
        P(None, "gx", None),
        P(None, "gx"),
        P(None, "gy"),
        P("gx", None),
        P("gy", None),
        P(),
        P(),
    )
    return jax.shard_map(
        body,
        mesh=mesh,
        in_specs=placed,
        out_specs=(P(("gx", "gy"), None), P("gy", None), P("gx", None, "gy"), P()),
        check_vma=False,
    )
```

```python
import functools
import math

import jax
import jax.numpy as jnp
from jax import lax
from jax.experimental import pallas as pl
from jax.experimental.pallas import tpu as pltpu
from jax.sharding import PartitionSpec as P


HIGHEST = lax.Precision.HIGHEST
F32 = jnp.float32
BF16 = jnp.bfloat16


MIB = 1 << 20
WIDE_LIMIT = 58 * MIB


def exchange(value, axis, bit):
    size = lax.axis_size(axis)
    return lax.ppermute(value, axis, [(i, i ^ bit) for i in range(size)])


def halves(value, bit, axis):
    size = value.shape[0] // 2
    upper = (lax.axis_index(axis) & bit) // bit
    keep = lax.dynamic_slice_in_dim(value, upper * size, size, 0)
    send = lax.dynamic_slice_in_dim(value, (1 - upper) * size, size, 0)
    return keep, send


def joined(mine, other, bit, axis):
    upper = (lax.axis_index(axis) & bit) != 0
    return jnp.where(upper, jnp.concatenate([other, mine]), jnp.concatenate([mine, other]))


def bits_of(size):
    return [1 << i for i in range(size.bit_length() - 1)]


HBM = pl.BlockSpec(memory_space=pltpu.HBM)
VMEM = pl.BlockSpec(memory_space=pltpu.VMEM)


def split(value):
    high = value.astype(BF16)
    return high, (value - high.astype(F32)).astype(BF16)


def mode_one_kernel(groups, snap_hbm, test_hbm, *refs):
    outs = refs[: len(groups)]
    snap, test, snap_sem, test_sem = refs[len(groups) :]
    along = lax.axis_index("gy")
    moments, block = snap.shape[1:3]
    rank = outs[0].shape[2]
    lanes = [slice(t * rank, (t + 1) * rank) for t in range(moments)]
    test_copies = [
        pltpu.make_async_copy(test_hbm.at[t], test.at[:, lanes[t]], test_sem.at[t])
        for t in range(moments)
    ]
    copies = []
    for index, name in enumerate(name for group in groups for name in group):
        start = pl.multiple_of((along ^ name) * block, block)
        copies.append(
            pltpu.make_async_copy(
                snap_hbm.at[:, pl.ds(start, block), :], snap.at[index], snap_sem.at[index]
            )
        )
    for copy in test_copies + copies:
        copy.start()
    for copy in test_copies:
        copy.wait()
    index = 0
    for group, out in zip(groups, outs):
        for i in range(len(group)):
            copies[index].wait()
            both = [
                jnp.dot(snap[index, t], test[...], preferred_element_type=F32)
                for t in range(moments)
            ]
            total = both[0][:, lanes[0]]
            for t in range(1, moments):
                total += both[t][:, lanes[t]]
            out[i] = total
            index += 1


def mode_one_blocks(groups, snapshots, test, block):
    moments, _, cols = snapshots.shape
    rank = test.shape[2]
    count = sum(len(group) for group in groups)
    return pl.pallas_call(
        functools.partial(mode_one_kernel, groups),
        in_specs=[HBM, HBM],
        out_specs=[VMEM] * len(groups),
        out_shape=[jax.ShapeDtypeStruct((len(group), block, rank), F32) for group in groups],
        scratch_shapes=[
            pltpu.VMEM((count, moments, block, cols), snapshots.dtype),
            pltpu.VMEM((cols, moments * rank), test.dtype),
            pltpu.SemaphoreType.DMA((count,)),
            pltpu.SemaphoreType.DMA((moments,)),
        ],
        cost_estimate=pl.CostEstimate(
            flops=4 * moments * count * block * cols * rank,
            bytes_accessed=4 * moments * count * block * cols,
            transcendentals=0,
        ),
        compiler_params=pltpu.CompilerParams(vmem_limit_bytes=WIDE_LIMIT),
        name="mode_one",
    )(snapshots, test)


def load_snapshots(order, snap_hbm, snap, sems):
    rows = snap.shape[1]
    pieces = sems.shape[1]
    block = rows // pieces
    copies = {}
    for n, t in enumerate(order):
        for i in range(pieces):
            span = pl.ds(i * block, block)
            copies[n, i] = pltpu.make_async_copy(
                snap_hbm.at[t, span, :], snap.at[n, span, :], sems.at[n, i]
            )
            copies[n, i].start()
    return copies, block


def core_kernel(snap_hbm, row_ref, column_ref, sent_ref, kept_ref, snap, total, sems):
    rank = kept_ref.shape[2]
    upper = lax.axis_index("gx") & 1
    copies, block = load_snapshots((1 - upper, upper), snap_hbm, snap, sems)
    contract = (((1,), (1,)), ((), ()))
    for n, out_ref in enumerate((sent_ref, kept_ref)):
        for i in range(sems.shape[1]):
            copies[n, i].wait()
            span = slice(i * block, (i + 1) * block)
            term = jnp.dot(row_ref[:, span], snap[n, span, :], preferred_element_type=F32)
            if i == 0:
                total[...] = term
            else:
                total[...] += term
        high, low = split(total[...])
        for g in range(out_ref.shape[0]):
            columns = column_ref[g * rank : (g + 1) * rank, :]
            out_ref[g] = lax.dot_general(
                high, columns, contract, preferred_element_type=F32
            ) + lax.dot_general(low, columns, contract, preferred_element_type=F32)


def core_products(snapshots, row_sketch, column_sketch, rank):
    moments, rows, cols = snapshots.shape
    sketch = row_sketch.shape[0]
    half = jax.ShapeDtypeStruct((sketch // rank, sketch, rank), F32)
    return pl.pallas_call(
        core_kernel,
        in_specs=[HBM, VMEM, VMEM],
        out_specs=[VMEM, VMEM],
        out_shape=[half, half],
        scratch_shapes=[
            pltpu.VMEM((moments, rows, cols), snapshots.dtype),
            pltpu.VMEM((sketch, cols), F32),
            pltpu.SemaphoreType.DMA((moments, 2)),
        ],
        cost_estimate=pl.CostEstimate(
            flops=4 * moments * rows * cols * sketch,
            bytes_accessed=2 * moments * rows * cols,
            transcendentals=0,
        ),
        compiler_params=pltpu.CompilerParams(vmem_limit_bytes=WIDE_LIMIT),
        name="core_tile",
    )(snapshots, row_sketch, column_sketch)


def two_kernel(snap_hbm, test_ref, sent_ref, kept_ref, snap, factors, total, turned, sems):
    moments = snap.shape[0]
    size = kept_ref.shape[0]
    upper = lax.axis_index("gx") & 1
    copies, block = load_snapshots(range(moments), snap_hbm, snap, sems)
    for t in range(moments):
        factors[t] = test_ref[t].T
    for t in range(moments):
        for i in range(sems.shape[1]):
            copies[t, i].wait()
            span = slice(i * block, (i + 1) * block)
            term = jnp.dot(factors[t, :, span], snap[t, span, :], preferred_element_type=F32)
            if t == 0 and i == 0:
                total[...] = term
            else:
                total[...] += term
    turned[...] = total[...].T
    kept_ref[...] = turned[pl.ds(pl.multiple_of(upper * size, size), size), :]
    sent_ref[...] = turned[pl.ds(pl.multiple_of((1 - upper) * size, size), size), :]


def two_products(snapshots, two_test):
    moments, rows, cols = snapshots.shape
    rank = two_test.shape[2]
    half = jax.ShapeDtypeStruct((cols // 2, rank), F32)
    return pl.pallas_call(
        two_kernel,
        in_specs=[HBM, VMEM],
        out_specs=[VMEM, VMEM],
        out_shape=[half, half],
        scratch_shapes=[
            pltpu.VMEM((moments, rows, cols), snapshots.dtype),
            pltpu.VMEM((moments, rank, rows), BF16),
            pltpu.VMEM((rank, cols), F32),
            pltpu.VMEM((cols, rank), F32),
            pltpu.SemaphoreType.DMA((moments, 2)),
        ],
        cost_estimate=pl.CostEstimate(
            flops=4 * moments * rows * cols * rank,
            bytes_accessed=2 * moments * rows * cols,
            transcendentals=0,
        ),
        compiler_params=pltpu.CompilerParams(vmem_limit_bytes=WIDE_LIMIT),
        name="two_tile",
    )(snapshots, two_test)


def gram_kernel(
    names, mine_ref, other_ref, core_ref, core_moved_ref, old_hbm, rows_ref, gram_ref, old, sem
):
    along = lax.axis_index("gy")
    count, block, rank = mine_ref.shape
    copies = []
    for i, name in enumerate(names):
        start = pl.multiple_of((along ^ name) * block, block)
        copies.append(
            pltpu.make_async_copy(old_hbm.at[pl.ds(start, block), :], old.at[i], sem.at[i])
        )
    for copy in copies:
        copy.start()
    gram = jnp.zeros((rank, rank), F32)
    for i in range(count):
        copies[i].wait()
        value = mine_ref[i] + other_ref[count - 1 - i] + old[i]
        rows_ref[i * block : (i + 1) * block, :] = value
        gram += lax.dot_general(
            value, value, (((0,), (0,)), ((), ())), precision=HIGHEST, preferred_element_type=F32
        )
    gram_ref[...] = gram
    rows_ref[count * block :, :] = core_ref[...] + core_moved_ref[...]


def finish_rows(names, mine, other, core_block, core_moved, old):
    count, block, rank = mine.shape
    return pl.pallas_call(
        functools.partial(gram_kernel, names),
        in_specs=[VMEM] * 4 + [HBM],
        out_specs=[VMEM, VMEM],
        out_shape=[
            jax.ShapeDtypeStruct((count * block + core_block.shape[0], rank), F32),
            jax.ShapeDtypeStruct((rank, rank), F32),
        ],
        scratch_shapes=[pltpu.VMEM((count, block, rank), F32), pltpu.SemaphoreType.DMA((count,))],
        compiler_params=pltpu.CompilerParams(vmem_limit_bytes=8 * MIB),
        name="gram",
    )(mine, other, core_block, core_moved, old)


def invert_factor(gram, inverse_ref):
    size = gram.shape[0]
    groups = size // 8
    left = [gram[8 * q : 8 * q + 8, :] for q in range(groups)]
    row = lax.broadcasted_iota(jnp.int32, (8, size), 0)
    column = lax.broadcasted_iota(jnp.int32, (8, size), 1)
    right = [jnp.where(column == row + 8 * q, 1.0, 0.0).astype(F32) for q in range(groups)]

    def spread(value, i):
        return jnp.broadcast_to(value[i : i + 1, :], (8, size))

    def column_of(value, c):
        return jnp.broadcast_to(value[:, c : c + 1], (8, size))

    for p in range(groups):
        panel = [column_of(left[p], 8 * p + k) for k in range(8)]
        pivots = jnp.ones((8, size), F32)
        inverses = []
        for j in range(8):
            pivot = spread(panel[j], j)
            pivots = jnp.where(row == j, pivot, pivots)
            inverses.append(1.0 / pivot)
            factor = jnp.where(row > j, panel[j] * inverses[j], 0.0)
            for k in range(j + 1, 8):
                panel[k] = panel[k] - factor * spread(panel[k], j)
            left[p] = left[p] - factor * spread(left[p], j)
            right[p] = right[p] - factor * spread(right[p], j)
        inverse_ref[8 * p : 8 * p + 8, :] = right[p] * lax.rsqrt(pivots)
        upper = {(k, j): spread(panel[k], j) for j in range(8) for k in range(j + 1, 8)}
        left_rows = [spread(left[p], j) for j in range(8)]
        right_rows = [spread(right[p], j) for j in range(8)]
        for q in range(p + 1, groups):
            below = [column_of(left[q], 8 * p + k) for k in range(8)]
            for j in range(8):
                factor = below[j] * inverses[j]
                for k in range(j + 1, 8):
                    below[k] = below[k] - factor * upper[k, j]
                left[q] = left[q] - factor * left_rows[j]
                right[q] = right[q] - factor * right_rows[j]


def product(a, b):
    contract = (((1,), (1,)), ((), ()))
    (a_high, a_low), (b_high, b_low) = split(a), split(b)
    total = lax.dot_general(a_high, b_low, contract, preferred_element_type=F32)
    total += lax.dot_general(a_low, b_high, contract, preferred_element_type=F32)
    return total + lax.dot_general(a_high, b_high, contract, preferred_element_type=F32)


def finish_kernel(root_rows, names, places, sizes, gram_ref, moved_ref, snap_hbm, *refs):
    parts = len(sizes)
    pieces = refs[:parts]
    own_ref = refs[parts]
    inverse, turned, low, total, snap, sems = refs[-6:]
    outs = refs[parts + 1 : -6]
    along, across = lax.axis_index("gy"), lax.axis_index("gx")
    moments, count, block, _ = snap.shape
    copies = {}
    for t in range(moments):
        for i, name in enumerate(names):
            start = pl.multiple_of((along ^ name) * block, block)
            copies[t, i] = pltpu.make_async_copy(
                snap_hbm.at[t, pl.ds(start, block), :], snap.at[t, i], sems.at[t, i]
            )
            copies[t, i].start()
    invert_factor(gram_ref[...] + moved_ref[...], inverse)
    share = inverse.shape[0] // len(places)
    for k, place in enumerate(places):
        start = pl.multiple_of((across ^ place) * share, share)
        turned[k * share : (k + 1) * share, :] = inverse[pl.ds(start, share), :]
    at = 0
    for piece, size in zip(pieces, sizes):
        low[:, at : at + size] = (root_rows * product(turned[...], piece[:size, :])).astype(BF16)
        at += size
    for t in range(moments):
        for i in range(count):
            copies[t, i].wait()
            term = jnp.dot(
                low[:, i * block : (i + 1) * block], snap[t, i], preferred_element_type=F32
            )
            if i == 0:
                total[...] = term
            else:
                total[...] += term
        sent_ref, passed_ref, kept_ref = outs[3 * t : 3 * t + 3]
        shares = len(places) // 2
        kept_ref[...] = total[:share, :]
        for k in range(1, shares):
            passed_ref[k - 1] = total[k * share : (k + 1) * share, :]
        for k in range(shares):
            sent_ref[k] = total[(shares + k) * share : (shares + k + 1) * share, :]
    own_ref[...] = root_rows * product(pieces[0][:block, :], inverse[...])


def finish(names, places, gram, moved, snapshots, pieces, sizes, root_rows):
    rank = gram.shape[0]
    moments, rows, cols = snapshots.shape
    block = rows // len(names)
    share = rank // len(places)
    half = len(places) // 2
    shapes = [jax.ShapeDtypeStruct((block, rank), F32)]
    for _ in range(moments):
        shapes += [
            jax.ShapeDtypeStruct((half, share, cols), F32),
            jax.ShapeDtypeStruct((half - 1, share, cols), F32),
            jax.ShapeDtypeStruct((share, cols), F32),
        ]
    return pl.pallas_call(
        functools.partial(finish_kernel, root_rows, names, places, sizes),
        in_specs=[VMEM, VMEM, HBM] + [VMEM] * len(pieces),
        out_specs=[VMEM] * len(shapes),
        out_shape=shapes,
        scratch_shapes=[
            pltpu.VMEM((rank, rank), F32),
            pltpu.VMEM((rank, rank), F32),
            pltpu.VMEM((rank, rows), BF16),
            pltpu.VMEM((rank, cols), F32),
            pltpu.VMEM((moments, len(names), block, cols), snapshots.dtype),
            pltpu.SemaphoreType.DMA((moments, len(names))),
        ],
        cost_estimate=pl.CostEstimate(
            flops=8 * rows * cols * rank, bytes_accessed=4 * rows * cols, transcendentals=0
        ),
        compiler_params=pltpu.CompilerParams(vmem_limit_bytes=WIDE_LIMIT),
        name="finish",
    )(gram, moved, snapshots, *pieces)


def body(
    snapshots,
    mode_one_test,
    mode_two_test,
    row_sketch,
    column_sketch,
    old_mode_one,
    old_mode_two,
    old_core,
    time_mix,
):
    moments, tile_rows, _ = snapshots.shape
    rank = mode_one_test.shape[2]
    wide, deep = lax.axis_size("gx"), lax.axis_size("gy")
    bits_x, bits_y = bits_of(wide), bits_of(deep)
    root_rows = math.sqrt(tile_rows * wide)
    block = tile_rows // deep

    scatter_bits, last = bits_y[:-1], bits_y[-1]
    first, rest = scatter_bits[0], scatter_bits[1:]

    names = range(deep)
    early = [j for j in names if j & first and j & rest[0]]
    late = [j for j in names if j & first and not j & rest[0]]
    high_names = [j ^ first for j in early]
    low_names = [j ^ first for j in late]
    (early_part,) = mode_one_blocks([early], snapshots, mode_one_test, block)
    early_sent = exchange(early_part, "gy", first)
    after_early = lax.optimization_barrier((snapshots, early_part))[0]
    late_part, high, low = mode_one_blocks(
        [late, high_names, low_names], after_early, mode_one_test, block
    )
    late_sent = exchange(late_part, "gy", first)
    high = high + early_sent
    side_input = lax.optimization_barrier((snapshots, high))[0]
    low = low + late_sent
    low = low + exchange(high, "gy", rest[0])
    for bit in rest[1:]:
        keep = [n for n, j in enumerate(low_names) if not j & bit]
        send = [low_names.index(low_names[n] ^ bit) for n in keep]
        moved = exchange(jnp.stack([low[n] for n in send]), "gy", bit)
        low = jnp.stack([low[n] for n in keep]) + moved
        low_names = [low_names[n] for n in keep]
    other = exchange(low, "gy", last)

    sent, kept = core_products(side_input, row_sketch, column_sketch, rank)
    core_shape = (2,) + kept.shape
    value = (kept + exchange(sent, "gx", bits_x[0])).reshape(-1, rank)
    two_input = lax.optimization_barrier((snapshots, kept))[0]
    sent, two = two_products(two_input, mode_two_test)
    for bit in bits_x[1:]:
        keep, send = halves(value, bit, "gx")
        value = keep + exchange(send, "gx", bit)
    two = two + exchange(sent, "gx", bits_x[0])
    for bit in bits_x[1:]:
        two = two + exchange(two, "gx", bit)
    around = [bit for bit in bits_y if bit != scatter_bits[-1]]
    for bit in around[:-2]:
        value = value + exchange(value, "gy", bit)
    core_moved = exchange(value, "gy", around[-2])
    rows_and_core, gram = finish_rows(low_names, low, other, value, core_moved, old_mode_one)
    core_at = len(low_names) * block

    for bit in bits_x:
        gram = gram + exchange(gram, "gx", bit)
    for n, bit in enumerate(scatter_bits):
        gram_moved = exchange(gram, "gy", bit)
        if n < len(scatter_bits) - 1:
            gram = gram + gram_moved

    one, next_one = scatter_bits[-1], scatter_bits[0]
    own = rows_and_core
    by_one = exchange(own, "gy", one)
    by_next = exchange(own[:core_at], "gy", next_one)
    corner_0 = exchange(by_one[:block], "gy", next_one)
    corner_1 = exchange(by_next[block:core_at], "gy", one)
    pieces = [own, by_one, by_next, corner_0, corner_1]
    sizes = [core_at, core_at, core_at, block, block]
    piece_names = list(low_names)
    piece_names += [j ^ one for j in low_names] + [j ^ next_one for j in low_names]
    piece_names += [low_names[0] ^ one ^ next_one, low_names[1] ^ one ^ next_one]
    for bit in scatter_bits[1:-1]:
        pieces = pieces + [exchange(p[:size], "gy", bit) for p, size in zip(pieces, sizes)]
        sizes = sizes + sizes
        piece_names = piece_names + [j ^ bit for j in piece_names]
    value = own[core_at:] + by_one[core_at:]
    value = value + exchange(value, "gy", around[-1])

    first_x = bits_x[0]
    places = [j for j in range(wide) if not j & first_x] + [j for j in range(wide) if j & first_x]
    shares = places[: wide // 2]
    basis_out, *parts = finish(
        piece_names, places, gram, gram_moved, snapshots, pieces, sizes, root_rows
    )
    projected = []
    for t in range(moments):
        sent, passed, kept = parts[3 * t : 3 * t + 3]
        moved = exchange(sent, "gx", first_x)
        kept = kept + moved[0]
        passed = passed + moved[1:]
        held = list(shares)
        for bit in bits_x[1:]:
            keep = [m for m, j in enumerate(held) if not j & bit]
            send = [held.index(held[m] ^ bit) for m in keep]
            send = jnp.stack([passed[m - 1] for m in send]).astype(BF16)
            moved = exchange(send, "gx", bit).astype(F32)
            kept = kept + moved[0]
            if len(keep) > 1:
                passed = jnp.stack([passed[m - 1] for m in keep[1:]]) + moved[1:]
            held = [held[m] for m in keep]
        projected.append(kept)
    projected = jnp.stack(projected, axis=1) / root_rows

    two_back = exchange(two, "gx", first_x)
    mode_two = old_mode_two + joined(two, two_back, first_x, "gx")
    for bit in reversed(bits_x):
        value = joined(value, exchange(value, "gx", bit), bit, "gx")
    stacked = value.reshape(core_shape)
    core = old_core
    for t in range(moments):
        term = jnp.concatenate(list(stacked[t]), axis=1)
        core = core + time_mix[:, t][:, None, None] * term
    return (basis_out, mode_two, projected, core)


def solution(mesh):
    placed = (
        P(None, "gx", "gy"),
        P(None, "gy", None),
        P(None, "gx", None),
        P(None, "gx"),
        P(None, "gy"),
        P("gx", None),
        P("gy", None),
        P(),
        P(),
    )

    return jax.shard_map(
        body,
        mesh=mesh,
        in_specs=placed,
        out_specs=(P(("gx", "gy"), None), P("gy", None), P("gx", None, "gy"), P()),
        check_vma=False,
    )
```

```python
import functools
import math

import jax
import jax.numpy as jnp
from jax import lax
from jax.experimental import pallas as pl
from jax.experimental.pallas import tpu as pltpu
from jax.sharding import PartitionSpec as P


HIGHEST = lax.Precision.HIGHEST
F32 = jnp.float32
BF16 = jnp.bfloat16


MIB = 1 << 20
WIDE_LIMIT = 56 * MIB


def exchange(value, axis, bit):
    size = lax.axis_size(axis)
    return lax.ppermute(value, axis, [(i, i ^ bit) for i in range(size)])


def halves(value, bit, axis):
    size = value.shape[0] // 2
    upper = (lax.axis_index(axis) & bit) // bit
    keep = lax.dynamic_slice_in_dim(value, upper * size, size, 0)
    send = lax.dynamic_slice_in_dim(value, (1 - upper) * size, size, 0)
    return keep, send


def joined(mine, other, bit, axis):
    upper = (lax.axis_index(axis) & bit) != 0
    return jnp.where(upper, jnp.concatenate([other, mine]), jnp.concatenate([mine, other]))


def bits_of(size):
    return [1 << i for i in range(size.bit_length() - 1)]


HBM = pl.BlockSpec(memory_space=pltpu.HBM)
VMEM = pl.BlockSpec(memory_space=pltpu.VMEM)


def split(value):
    high = value.astype(BF16)
    return high, (value - high.astype(F32)).astype(BF16)


def mode_one_kernel(groups, snap_hbm, test_hbm, *refs):
    outs = refs[: len(groups)]
    snap, test, snap_sem, test_sem = refs[len(groups) :]
    along = lax.axis_index("gy")
    moments, block = snap.shape[1:3]
    rank = outs[0].shape[2]
    lanes = [slice(t * rank, (t + 1) * rank) for t in range(moments)]
    test_copies = [
        pltpu.make_async_copy(test_hbm.at[t], test.at[:, lanes[t]], test_sem.at[t])
        for t in range(moments)
    ]
    copies = []
    for index, name in enumerate(name for group in groups for name in group):
        start = pl.multiple_of((along ^ name) * block, block)
        copies.append(
            pltpu.make_async_copy(
                snap_hbm.at[:, pl.ds(start, block), :], snap.at[index], snap_sem.at[index]
            )
        )
    for copy in test_copies + copies:
        copy.start()
    for copy in test_copies:
        copy.wait()
    index = 0
    for group, out in zip(groups, outs):
        for i in range(len(group)):
            copies[index].wait()
            both = [
                jnp.dot(snap[index, t], test[...], preferred_element_type=F32)
                for t in range(moments)
            ]
            total = both[0][:, lanes[0]]
            for t in range(1, moments):
                total += both[t][:, lanes[t]]
            out[i] = total
            index += 1


def mode_one_blocks(groups, snapshots, test, block):
    moments, _, cols = snapshots.shape
    rank = test.shape[2]
    count = sum(len(group) for group in groups)
    return pl.pallas_call(
        functools.partial(mode_one_kernel, groups),
        in_specs=[HBM, HBM],
        out_specs=[VMEM] * len(groups),
        out_shape=[jax.ShapeDtypeStruct((len(group), block, rank), F32) for group in groups],
        scratch_shapes=[
            pltpu.VMEM((count, moments, block, cols), snapshots.dtype),
            pltpu.VMEM((cols, moments * rank), test.dtype),
            pltpu.SemaphoreType.DMA((count,)),
            pltpu.SemaphoreType.DMA((moments,)),
        ],
        cost_estimate=pl.CostEstimate(
            flops=4 * moments * count * block * cols * rank,
            bytes_accessed=4 * moments * count * block * cols,
            transcendentals=0,
        ),
        compiler_params=pltpu.CompilerParams(vmem_limit_bytes=WIDE_LIMIT),
        name="mode_one",
    )(snapshots, test)


def load_snapshots(order, snap_hbm, snap, sems):
    rows = snap.shape[1]
    pieces = sems.shape[1]
    block = rows // pieces
    copies = {}
    for n, t in enumerate(order):
        for i in range(pieces):
            span = pl.ds(i * block, block)
            copies[n, i] = pltpu.make_async_copy(
                snap_hbm.at[t, span, :], snap.at[n, span, :], sems.at[n, i]
            )
            copies[n, i].start()
    return copies, block


def core_kernel(
    snap_hbm, row_hbm, column_hbm, sent_ref, kept_ref, row_ref, column_ref, snap, total, pair, sems
):
    rank = kept_ref.shape[2]
    upper = lax.axis_index("gx") & 1
    row_copy = pltpu.make_async_copy(row_hbm, row_ref, pair.at[0])
    column_copy = pltpu.make_async_copy(column_hbm, column_ref, pair.at[1])
    row_copy.start()
    copies, block = load_snapshots((1 - upper, upper), snap_hbm, snap, sems)
    column_copy.start()
    contract = (((1,), (1,)), ((), ()))
    row_copy.wait()
    for n, out_ref in enumerate((sent_ref, kept_ref)):
        for i in range(sems.shape[1]):
            copies[n, i].wait()
            span = slice(i * block, (i + 1) * block)
            term = jnp.dot(row_ref[:, span], snap[n, span, :], preferred_element_type=F32)
            if i == 0:
                total[...] = term
            else:
                total[...] += term
        high, low = split(total[...])
        if n == 0:
            column_copy.wait()
        for g in range(out_ref.shape[0]):
            columns = column_ref[g * rank : (g + 1) * rank, :]
            out_ref[g] = lax.dot_general(
                high, columns, contract, preferred_element_type=F32
            ) + lax.dot_general(low, columns, contract, preferred_element_type=F32)


def core_products(snapshots, row_sketch, column_sketch, rank):
    moments, rows, cols = snapshots.shape
    sketch = row_sketch.shape[0]
    half = jax.ShapeDtypeStruct((sketch // rank, sketch, rank), F32)
    return pl.pallas_call(
        core_kernel,
        in_specs=[HBM, HBM, HBM],
        out_specs=[VMEM, VMEM],
        out_shape=[half, half],
        scratch_shapes=[
            pltpu.VMEM(row_sketch.shape, row_sketch.dtype),
            pltpu.VMEM(column_sketch.shape, column_sketch.dtype),
            pltpu.VMEM((moments, rows, cols), snapshots.dtype),
            pltpu.VMEM((sketch, cols), F32),
            pltpu.SemaphoreType.DMA((2,)),
            pltpu.SemaphoreType.DMA((moments, 2)),
        ],
        cost_estimate=pl.CostEstimate(
            flops=4 * moments * rows * cols * sketch,
            bytes_accessed=2 * moments * rows * cols,
            transcendentals=0,
        ),
        compiler_params=pltpu.CompilerParams(vmem_limit_bytes=WIDE_LIMIT),
        name="core_tile",
    )(snapshots, row_sketch, column_sketch)


def two_kernel(
    snap_hbm, test_hbm, sent_ref, kept_ref, test, snap, factors, total, turned, test_sem, sems
):
    moments = snap.shape[0]
    size = kept_ref.shape[0]
    upper = lax.axis_index("gx") & 1
    test_copy = pltpu.make_async_copy(test_hbm, test, test_sem)
    test_copy.start()
    copies, block = load_snapshots(range(moments), snap_hbm, snap, sems)
    test_copy.wait()
    for t in range(moments):
        factors[t] = test[t].T
    for t in range(moments):
        for i in range(sems.shape[1]):
            copies[t, i].wait()
            span = slice(i * block, (i + 1) * block)
            term = jnp.dot(factors[t, :, span], snap[t, span, :], preferred_element_type=F32)
            if t == 0 and i == 0:
                total[...] = term
            else:
                total[...] += term
    turned[...] = total[...].T
    kept_ref[...] = turned[pl.ds(pl.multiple_of(upper * size, size), size), :]
    sent_ref[...] = turned[pl.ds(pl.multiple_of((1 - upper) * size, size), size), :]


def two_products(snapshots, two_test):
    moments, rows, cols = snapshots.shape
    rank = two_test.shape[2]
    half = jax.ShapeDtypeStruct((cols // 2, rank), F32)
    return pl.pallas_call(
        two_kernel,
        in_specs=[HBM, HBM],
        out_specs=[VMEM, VMEM],
        out_shape=[half, half],
        scratch_shapes=[
            pltpu.VMEM(two_test.shape, two_test.dtype),
            pltpu.VMEM((moments, rows, cols), snapshots.dtype),
            pltpu.VMEM((moments, rank, rows), BF16),
            pltpu.VMEM((rank, cols), F32),
            pltpu.VMEM((cols, rank), F32),
            pltpu.SemaphoreType.DMA,
            pltpu.SemaphoreType.DMA((moments, 2)),
        ],
        cost_estimate=pl.CostEstimate(
            flops=4 * moments * rows * cols * rank,
            bytes_accessed=2 * moments * rows * cols,
            transcendentals=0,
        ),
        compiler_params=pltpu.CompilerParams(vmem_limit_bytes=WIDE_LIMIT),
        name="two_tile",
    )(snapshots, two_test)


def gram_kernel(names, mine_ref, other_ref, old_hbm, rows_ref, gram_ref, old, sem):
    along = lax.axis_index("gy")
    count, block, rank = mine_ref.shape
    copies = []
    for i, name in enumerate(names):
        start = pl.multiple_of((along ^ name) * block, block)
        copies.append(
            pltpu.make_async_copy(old_hbm.at[pl.ds(start, block), :], old.at[i], sem.at[i])
        )
    for copy in copies:
        copy.start()
    gram = jnp.zeros((rank, rank), F32)
    for i in range(count):
        copies[i].wait()
        value = mine_ref[i] + other_ref[count - 1 - i] + old[i]
        rows_ref[i * block : (i + 1) * block, :] = value
        gram += lax.dot_general(
            value, value, (((0,), (0,)), ((), ())), precision=HIGHEST, preferred_element_type=F32
        )
    gram_ref[...] = gram


def finish_rows(names, mine, other, old):
    count, block, rank = mine.shape
    return pl.pallas_call(
        functools.partial(gram_kernel, names),
        in_specs=[VMEM, VMEM, HBM],
        out_specs=[VMEM, VMEM],
        out_shape=[
            jax.ShapeDtypeStruct((count * block, rank), F32),
            jax.ShapeDtypeStruct((rank, rank), F32),
        ],
        scratch_shapes=[pltpu.VMEM((count, block, rank), F32), pltpu.SemaphoreType.DMA((count,))],
        compiler_params=pltpu.CompilerParams(vmem_limit_bytes=8 * MIB),
        name="gram",
    )(mine, other, old)


def invert_factor(gram, inverse_ref):
    size = gram.shape[0]
    groups = size // 8
    left = [gram[8 * q : 8 * q + 8, :] for q in range(groups)]
    row = lax.broadcasted_iota(jnp.int32, (8, size), 0)
    column = lax.broadcasted_iota(jnp.int32, (8, size), 1)
    right = [jnp.where(column == row + 8 * q, 1.0, 0.0).astype(F32) for q in range(groups)]

    def spread(value, i):
        return jnp.broadcast_to(value[i : i + 1, :], (8, size))

    def column_of(value, c):
        return jnp.broadcast_to(value[:, c : c + 1], (8, size))

    for p in range(groups):
        panel = [column_of(left[p], 8 * p + k) for k in range(8)]
        pivots = jnp.ones((8, size), F32)
        inverses = []
        for j in range(8):
            pivot = spread(panel[j], j)
            pivots = jnp.where(row == j, pivot, pivots)
            inverses.append(1.0 / pivot)
            factor = jnp.where(row > j, panel[j] * inverses[j], 0.0)
            for k in range(j + 1, 8):
                panel[k] = panel[k] - factor * spread(panel[k], j)
            left[p] = left[p] - factor * spread(left[p], j)
            right[p] = right[p] - factor * spread(right[p], j)
        inverse_ref[8 * p : 8 * p + 8, :] = right[p] * lax.rsqrt(pivots)
        upper = {(k, j): spread(panel[k], j) for j in range(8) for k in range(j + 1, 8)}
        left_rows = [spread(left[p], j) for j in range(8)]
        right_rows = [spread(right[p], j) for j in range(8)]
        for q in range(p + 1, groups):
            below = [column_of(left[q], 8 * p + k) for k in range(8)]
            for j in range(8):
                factor = below[j] * inverses[j]
                for k in range(j + 1, 8):
                    below[k] = below[k] - factor * upper[k, j]
                left[q] = left[q] - factor * left_rows[j]
                right[q] = right[q] - factor * right_rows[j]


def product(a, b):
    contract = (((1,), (1,)), ((), ()))
    (a_high, a_low), (b_high, b_low) = split(a), split(b)
    total = lax.dot_general(a_high, b_low, contract, preferred_element_type=F32)
    total += lax.dot_general(a_low, b_high, contract, preferred_element_type=F32)
    return total + lax.dot_general(a_high, b_high, contract, preferred_element_type=F32)


def finish_kernel(root_rows, names, places, sizes, gram_ref, moved_ref, snap_hbm, *refs):
    parts = len(sizes)
    pieces = refs[:parts]
    own_ref = refs[parts]
    inverse, turned, low, total, snap, sems = refs[-6:]
    sent_ref, passed_ref, kept_ref = refs[parts + 1 : -6]
    along, across = lax.axis_index("gy"), lax.axis_index("gx")
    moments, count, block, _ = snap.shape
    copies = {}
    for t in range(moments):
        for i, name in enumerate(names):
            start = pl.multiple_of((along ^ name) * block, block)
            copies[t, i] = pltpu.make_async_copy(
                snap_hbm.at[t, pl.ds(start, block), :], snap.at[t, i], sems.at[t, i]
            )
            copies[t, i].start()
    invert_factor(gram_ref[...] + moved_ref[...], inverse)
    share = inverse.shape[0] // len(places)
    for k, place in enumerate(places):
        start = pl.multiple_of((across ^ place) * share, share)
        turned[k * share : (k + 1) * share, :] = inverse[pl.ds(start, share), :]
    at = 0
    for piece, size in zip(pieces, sizes):
        low[:, at : at + size] = (root_rows * product(turned[...], piece[:size, :])).astype(BF16)
        at += size
    for t in range(moments):
        for i in range(count):
            copies[t, i].wait()
            term = jnp.dot(
                low[:, i * block : (i + 1) * block], snap[t, i], preferred_element_type=F32
            )
            if i == 0:
                total[...] = term
            else:
                total[...] += term
        shares = len(places) // 2
        kept_ref[t] = total[:share, :]
        for k in range(1, shares):
            passed_ref[k - 1, t] = total[k * share : (k + 1) * share, :]
        for k in range(shares):
            sent_ref[k, t] = total[(shares + k) * share : (shares + k + 1) * share, :]
    own_ref[...] = root_rows * product(pieces[0][:block, :], inverse[...])


def finish(names, places, gram, moved, snapshots, pieces, sizes, root_rows):
    rank = gram.shape[0]
    moments, rows, cols = snapshots.shape
    block = rows // len(names)
    share = rank // len(places)
    half = len(places) // 2
    shapes = [
        jax.ShapeDtypeStruct((block, rank), F32),
        jax.ShapeDtypeStruct((half, moments, share, cols), F32),
        jax.ShapeDtypeStruct((half - 1, moments, share, cols), F32),
        jax.ShapeDtypeStruct((moments, share, cols), F32),
    ]
    return pl.pallas_call(
        functools.partial(finish_kernel, root_rows, names, places, sizes),
        in_specs=[VMEM, VMEM, HBM] + [VMEM] * len(pieces),
        out_specs=[VMEM] * len(shapes),
        out_shape=shapes,
        scratch_shapes=[
            pltpu.VMEM((rank, rank), F32),
            pltpu.VMEM((rank, rank), F32),
            pltpu.VMEM((rank, rows), BF16),
            pltpu.VMEM((rank, cols), F32),
            pltpu.VMEM((moments, len(names), block, cols), snapshots.dtype),
            pltpu.SemaphoreType.DMA((moments, len(names))),
        ],
        cost_estimate=pl.CostEstimate(
            flops=8 * rows * cols * rank, bytes_accessed=4 * rows * cols, transcendentals=0
        ),
        compiler_params=pltpu.CompilerParams(vmem_limit_bytes=WIDE_LIMIT),
        name="finish",
    )(gram, moved, snapshots, *pieces)


def total_kernel(root_rows, kept_ref, *refs):
    terms, out_ref = refs[:-1], refs[-1]
    for t in range(kept_ref.shape[0]):
        value = kept_ref[t]
        for term in terms:
            value = value + term[0, t].astype(F32)
        out_ref[:, t, :] = value / root_rows


def total_projection(kept, terms, root_rows):
    moments, share, cols = kept.shape
    return pl.pallas_call(
        functools.partial(total_kernel, root_rows),
        in_specs=[VMEM] * (1 + len(terms)),
        out_specs=VMEM,
        out_shape=jax.ShapeDtypeStruct((share, moments, cols), F32),
        compiler_params=pltpu.CompilerParams(vmem_limit_bytes=8 * MIB),
        name="total",
    )(kept, *terms)


def body(
    snapshots,
    mode_one_test,
    mode_two_test,
    row_sketch,
    column_sketch,
    old_mode_one,
    old_mode_two,
    old_core,
    time_mix,
):
    moments, tile_rows, _ = snapshots.shape
    rank = mode_one_test.shape[2]
    wide, deep = lax.axis_size("gx"), lax.axis_size("gy")
    bits_x, bits_y = bits_of(wide), bits_of(deep)
    root_rows = math.sqrt(tile_rows * wide)
    block = tile_rows // deep

    scatter_bits, last = bits_y[:-1], bits_y[-1]
    first, rest = scatter_bits[0], scatter_bits[1:]

    names = range(deep)
    early = [j for j in names if j & first and j & rest[0]]
    late = [j for j in names if j & first and not j & rest[0]]
    high_names = [j ^ first for j in early]
    low_names = [j ^ first for j in late]
    (early_part,) = mode_one_blocks([early], snapshots, mode_one_test, block)
    early_sent = exchange(early_part, "gy", first)
    after_early = lax.optimization_barrier((snapshots, early_part))[0]
    late_part, high, low = mode_one_blocks(
        [late, high_names, low_names], after_early, mode_one_test, block
    )
    late_sent = exchange(late_part, "gy", first)
    high = high + early_sent
    side_input = lax.optimization_barrier((snapshots, high))[0]
    low = low + late_sent
    low = low + exchange(high, "gy", rest[0])
    for bit in rest[1:]:
        keep = [n for n, j in enumerate(low_names) if not j & bit]
        send = [low_names.index(low_names[n] ^ bit) for n in keep]
        moved = exchange(jnp.stack([low[n] for n in send]), "gy", bit)
        low = jnp.stack([low[n] for n in keep]) + moved
        low_names = [low_names[n] for n in keep]
    other = exchange(low, "gy", last)

    sent, kept = core_products(side_input, row_sketch, column_sketch, rank)
    core_shape = (2,) + kept.shape
    value = (kept + exchange(sent, "gx", bits_x[0])).reshape(-1, rank)
    two_input = lax.optimization_barrier((snapshots, kept))[0]
    sent, two = two_products(two_input, mode_two_test)
    for bit in bits_x[1:]:
        keep, send = halves(value, bit, "gx")
        value = keep + exchange(send, "gx", bit)
    two = two + exchange(sent, "gx", bits_x[0])
    for bit in bits_x[1:]:
        two = two + exchange(two, "gx", bit)
    around = [bit for bit in bits_y if bit != scatter_bits[-1]]
    for bit in around[:-1]:
        value = value + exchange(value, "gy", bit)
    own, gram = finish_rows(low_names, low, other, old_mode_one)
    core_at = len(low_names) * block

    for bit in bits_x:
        gram = gram + exchange(gram, "gx", bit)
    for n, bit in enumerate(scatter_bits):
        gram_moved = exchange(gram, "gy", bit)
        if n < len(scatter_bits) - 1:
            gram = gram + gram_moved

    one, next_one = scatter_bits[-1], scatter_bits[0]
    by_one = exchange(own, "gy", one)
    by_next = exchange(own, "gy", next_one)
    corner_0 = exchange(by_one[:block], "gy", next_one)
    corner_1 = exchange(by_next[block:], "gy", one)
    pieces = [own, by_one, by_next, corner_0, corner_1]
    sizes = [core_at, core_at, core_at, block, block]
    piece_names = list(low_names)
    piece_names += [j ^ one for j in low_names] + [j ^ next_one for j in low_names]
    piece_names += [low_names[0] ^ one ^ next_one, low_names[1] ^ one ^ next_one]
    for bit in scatter_bits[1:-1]:
        pieces = pieces + [exchange(p[:size], "gy", bit) for p, size in zip(pieces, sizes)]
        sizes = sizes + sizes
        piece_names = piece_names + [j ^ bit for j in piece_names]
    value = value + exchange(value, "gy", one)
    value = value + exchange(value, "gy", around[-1])

    first_x = bits_x[0]
    places = [j for j in range(wide) if not j & first_x] + [j for j in range(wide) if j & first_x]
    shares = places[: wide // 2]
    basis_out, sent, passed, kept = finish(
        piece_names, places, gram, gram_moved, snapshots, pieces, sizes, root_rows
    )
    moved = exchange(sent, "gx", first_x)
    terms = [moved]
    passed = passed + moved[1:]
    held = list(shares)
    for bit in bits_x[1:]:
        keep = [m for m, j in enumerate(held) if not j & bit]
        send = [held.index(held[m] ^ bit) for m in keep]
        send = jnp.stack([passed[m - 1] for m in send]).astype(BF16)
        moved = exchange(send, "gx", bit)
        terms.append(moved)
        if len(keep) > 1:
            passed = jnp.stack([passed[m - 1] for m in keep[1:]]) + moved[1:].astype(F32)
        held = [held[m] for m in keep]
    projected = total_projection(kept, terms, root_rows)

    two_back = exchange(two, "gx", first_x)
    mode_two = old_mode_two + joined(two, two_back, first_x, "gx")
    for bit in reversed(bits_x):
        value = joined(value, exchange(value, "gx", bit), bit, "gx")
    stacked = value.reshape(core_shape)
    core = old_core
    for t in range(moments):
        term = jnp.concatenate(list(stacked[t]), axis=1)
        core = core + time_mix[:, t][:, None, None] * term
    return (basis_out, mode_two, projected, core)


def solution(mesh):
    placed = (
        P(None, "gx", "gy"),
        P(None, "gy", None),
        P(None, "gx", None),
        P(None, "gx"),
        P(None, "gy"),
        P("gx", None),
        P("gy", None),
        P(),
        P(),
    )

    return jax.shard_map(
        body,
        mesh=mesh,
        in_specs=placed,
        out_specs=(P(("gx", "gy"), None), P("gy", None), P("gx", None, "gy"), P()),
        check_vma=False,
    )
```
